32 devices in a mesh: grp: 2 (over x), chol: 16 (over z, y, core).
Axes of the slice: x: 2, y: 2, z: 4, core: 2. Of those that a mesh axis runs over, the one named last changes fastest.
Arguments:
- walkers: bfloat16 [1024, 64, 256], P(('grp', 'chol')), parts along dimension 0, may hold values from -6 to 6
- fields: bfloat16 [1024, 1024], P(('grp', 'chol')), parts along dimension 0, may hold values from -6 to 6
- chol_vectors: bfloat16 [1024, 256, 256], P(None, 'chol'), may hold values from -0.375 to 0.375
- rotated: bfloat16 [1024, 64, 256], P(None, 'chol'), may hold values from -0.046875 to 0.046875
- send_walker: int32 [32, 16, 2], P(('grp', 'chol')), parts along dimension 0, may hold values from -1 to 31, as said below
- slot_row: int32 [1024], P(('grp', 'chol')), parts along dimension 0, may hold values from 0 to 31, as said below
Outputs:
- new_walkers: bfloat16 [1024, 64, 256], P(('grp', 'chol')), parts along dimension 0
- force_bias: float32 [1024, 1024], P(('grp', 'chol')), parts along dimension 0
The draws below stay inside these ranges and needn't reach their ends.
There are 2 independent parts, one for each index of `grp`. The reference program is written for one: setup_inputs(seed, part) draws one part's arguments, and reference() takes and returns one part's arrays. A program takes and returns all parts, laid end to end along the dimension named above; an argument that names none is the same for every part. Nothing has to cross between parts.
Inputs may be any that keep to these rules, and one draw needn't show every extreme that they name: `send_walker`: entry [s, d, c] is the index, among the 32 walkers of block s, of the walker that block s sends as its c-th one to block d, or -1 where it sends none; indices of one [s, d] row come first, -1 after. Some pair of blocks uses all 2 entries. `slot_row`: for every slot of block d, s * 2 + c names a valid entry [s, d, c] of send_walker, and every valid entry is named by exactly one slot of block d.
All inputs are finite; a program needn't handle non-finite values.
Results may differ from the reference program's by a relative error of at most 0.0075.
Values may be sent and summed in bfloat16 or wider, within the bound.
A program may use at most 64 MiB of HBM per device.

```python
import math
import jax
import jax.numpy as jnp
from jax import lax

M = 256
N = 64
NCHOL = 1024
CAP = 2
W_DEV = 32
BLOCKS = 16
WALKERS = 512


def branch_plan(key):
    base = jax.random.fold_in(key, 4111)
    offset = jax.random.randint(jax.random.fold_in(base, 1), (), 0, BLOCKS)
    dest_keys = jax.random.split(jax.random.fold_in(base, 2), BLOCKS)

    def one_dest(dest_key, dest):
        key_a, key_b, key_c = jax.random.split(dest_key, 3)
        doubled = (dest + offset) % BLOCKS
        order = jax.random.permutation(key_a, 2 * (BLOCKS - 1)) % (BLOCKS - 1)
        others = jnp.where(order >= doubled, order + 1, order)[:W_DEV - 2]
        sources = jnp.concatenate([jnp.stack([doubled, doubled]), others]).astype(jnp.int32)
        sources = sources[jax.random.permutation(key_b, W_DEV)]
        walker_index = jax.random.randint(key_c, (W_DEV,), 0, W_DEV).astype(jnp.int32)
        positions = jnp.arange(W_DEV, dtype=jnp.int32)
        same = (sources[:, None] == sources[None, :]) & (positions[None, :] < positions[:, None])
        rank = jnp.sum(same.astype(jnp.int32), axis=1).astype(jnp.int32)
        return (sources, rank, walker_index)
    sources, rank, walker_index = jax.vmap(one_dest)(dest_keys, jnp.arange(BLOCKS, dtype=jnp.int32))
    dest_grid = jnp.broadcast_to(jnp.arange(BLOCKS, dtype=jnp.int32)[:, None], (BLOCKS, W_DEV))
    table = jnp.full((BLOCKS, BLOCKS, CAP), -1, jnp.int32)
    table = table.at[sources.reshape(-1), dest_grid.reshape(-1), rank.reshape(-1)].set(walker_index.reshape(-1))
    rows = (sources * CAP + rank).reshape(-1).astype(jnp.int32)
    return (table, rows)


def draw_send_walker(key, part):
    return branch_plan(key)[0]


def draw_slot_row(key, part):
    return branch_plan(key)[1]


def block_scale(rng, shape, pieces, least, largest):
    loudness = 1.0
    for axis_at, blocks in pieces:
        steps = jax.random.uniform(jax.random.fold_in(jax.random.fold_in(rng, 6), axis_at), (blocks,), jnp.float32, least / len(pieces), largest / len(pieces))
        loudness = loudness * jnp.repeat(jnp.exp(steps), shape[axis_at] // blocks).reshape((-1,) + (1,) * (len(shape) - 1 - axis_at))
    return loudness


def bell_draw(key, shape, spread, bound, pieces=(), kind=jnp.bfloat16):
    array = jax.random.normal(key, shape, jnp.float32) * spread
    if len(pieces) > 0:
        array = block_scale(key, shape, pieces, -0.22, 0.18) * array
    return jnp.clip(array, min=-bound, max=bound).astype(kind)


def setup_inputs(seed: int = 0, part: int = 0) -> dict:
    key_list = jax.random.split(jax.random.key(seed), 7)
    part_splits = jax.random.split(jax.random.fold_in(key_list[6], part), 7)
    walkers = bell_draw(part_splits[0], (WALKERS, N, M), 1.0, 6.0, ((0, 16),))
    fields = bell_draw(part_splits[1], (WALKERS, NCHOL), 1.0, 6.0, ((0, 16),))
    chol_vectors = bell_draw(key_list[2], (NCHOL, M, M), M ** -0.5, 0.375, ((1, 16),))
    rotated = bell_draw(key_list[3], (NCHOL, N, M), (N * M) ** -0.5, 0.046875, ((1, 16),))
    send_walker = draw_send_walker(jax.random.fold_in(jax.random.fold_in(key_list[6], part), 71), part)
    slot_row = draw_slot_row(jax.random.fold_in(jax.random.fold_in(key_list[6], part), 71), part)
    return dict(walkers=walkers, fields=fields, chol_vectors=chol_vectors, rotated=rotated, send_walker=send_walker, slot_row=slot_row)


field_scale = 1.5

def reference(walkers, fields, chol_vectors, rotated, send_walker, slot_row):
    dest = jnp.arange(WALKERS, dtype=jnp.int32) // W_DEV
    source = (slot_row // CAP).astype(jnp.int32)
    rank = (slot_row % CAP).astype(jnp.int32)
    local_index = send_walker[source, dest, rank].astype(jnp.int32)
    parent = (source * W_DEV + local_index).astype(jnp.int32)
    branched = walkers[parent]
    chol_flat = chol_vectors.reshape(NCHOL, M * M)
    rot_flat = rotated.reshape(NCHOL, N * M)
    scale = field_scale / math.sqrt(NCHOL)

    def propagate(blocks):
        field_rows, phi_block = blocks
        operator = (jnp.dot(field_rows, chol_flat, preferred_element_type=jnp.float32) * scale).astype(jnp.bfloat16)
        operator = operator.reshape(W_DEV, M, M)
        total = phi_block.astype(jnp.float32)
        term = phi_block
        for degree in range(1, 6):
            product = jnp.einsum('waj,wij->wai', term.astype(jnp.float32), operator.astype(jnp.float32))
            term = (product / degree).astype(jnp.bfloat16)
            total = total + term.astype(jnp.float32)
        new_block = total.astype(jnp.bfloat16)
        bias = lax.dot_general(new_block.reshape(W_DEV, N * M), rot_flat, (((1,), (1,)), ((), ())), preferred_element_type=jnp.float32)
        return (new_block, bias)
    new_all, bias_all = lax.map(propagate, (fields.reshape(BLOCKS, W_DEV, NCHOL), branched.reshape(BLOCKS, W_DEV, N, M)))
    return (new_all.reshape(WALKERS, N, M), bias_all.reshape(WALKERS, NCHOL))
```

```python
import functools
import math

import jax
import jax.numpy as jnp
from jax import lax
from jax.experimental import pallas as pl
from jax.experimental.pallas import tpu as pltpu
from jax.sharding import PartitionSpec as P

field_scale = 1.5
chunk_slots = 16
degrees = 5
MESH = pl.DeviceIdType.MESH


def exchange(me, blocks, send, recv, chunk, send_sem, recv_sem):
    def step(k, carry):
        peer = lax.rem(me + k, blocks)
        pltpu.make_async_remote_copy(
            src_ref=send.at[chunk, peer],
            dst_ref=recv.at[chunk, me],
            send_sem=send_sem.at[chunk],
            recv_sem=recv_sem.at[chunk],
            device_id={"chol": peer},
            device_id_type=MESH,
        ).start()
        return carry

    lax.fori_loop(1, blocks, step, 0)
    recv[chunk, me] = send[chunk, me]


def arrived(blocks, recv, chunk, sem):
    whole = recv.at[chunk, pl.ds(0, blocks - 1)]
    pltpu.make_async_copy(whole, whole, sem.at[chunk]).wait()


def kernel(
    dims,
    send_walker,
    slot_row,
    walkers,
    fields,
    chol,
    rotated,
    new_walkers,
    force_bias,
    br_send,
    br_recv,
    op_send,
    op_recv,
    op_rows,
    totals,
    nw_send,
    nw_recv,
    fb_send,
    fb_recv,
    send_sems,
    recv_sems,
):
    blocks, chunks, width, cap, rows, elec = dims
    slots, electrons, orbitals = walkers.shape
    nchol = rotated.shape[0]
    halves = orbitals // 128
    me = lax.axis_index("chol")

    barrier = pltpu.get_barrier_semaphore()

    def greet(k, carry):
        pl.semaphore_signal(
            barrier, inc=1, device_id={"chol": lax.rem(me + k, blocks)}, device_id_type=MESH
        )
        return carry

    lax.fori_loop(1, blocks, greet, 0)

    def pick(d, carry):
        for c in range(cap):
            br_send[0, d, c] = walkers[jnp.maximum(send_walker[d * cap + c], 0)]
        return carry

    lax.fori_loop(0, blocks, pick, 0)
    pl.semaphore_wait(barrier, blocks - 1)
    exchange(me, blocks, br_send, br_recv, 0, send_sems.at[0], recv_sems.at[0])

    scale = field_scale / math.sqrt(nchol)
    cols = rows * orbitals
    tile = min(512, cols)

    @pl.loop(0, cols // tile)
    def _(n):
        at = pl.ds(pl.multiple_of(n * tile, tile), tile)
        part = jnp.dot(fields[...], chol[:, at], preferred_element_type=jnp.float32) * scale
        op_send[:, :, :, at] = part.astype(jnp.bfloat16).reshape(chunks, blocks, width, tile)

    def send_operators(q):
        exchange(me, blocks, op_send, op_recv, q, send_sems.at[1], recv_sems.at[1])

    def taylor(q):
        def spread(s, carry):
            block = op_recv[q, s].astype(jnp.float32)
            for r in range(rows):
                for h in range(halves):
                    low = r * orbitals + h * 128
                    op_rows[h, pl.ds(s * rows + r, width, stride=orbitals), :] = block[
                        :, low : low + 128
                    ]
            return carry

        lax.fori_loop(0, blocks, spread, 0)
        group = 4

        @pl.loop(0, width // group)
        def _(g):
            ops, terms, sums = [], [], []
            for u in range(group):
                w = g * group + u
                first = pl.ds(pl.multiple_of(w * orbitals, orbitals), orbitals)
                ops.append(
                    jnp.concatenate([op_rows[h, first, :] for h in range(halves)], axis=1).astype(
                        jnp.bfloat16
                    )
                )
                row = slot_row[q * width + w]
                terms.append(br_recv[0, row // cap, row % cap])
                sums.append(terms[u].astype(jnp.float32))
            for degree in range(1, degrees + 1):
                for u in range(group):
                    product = lax.dot_general(
                        terms[u],
                        ops[u],
                        (((1,), (1,)), ((), ())),
                        preferred_element_type=jnp.float32,
                    )
                    terms[u] = (product * (1.0 / degree)).astype(jnp.bfloat16)
                    sums[u] = sums[u] + terms[u].astype(jnp.float32)
            for u in range(group):
                w = g * group + u
                new_walkers[q * width + w] = sums[u].astype(jnp.bfloat16)
                place = pl.ds(pl.multiple_of(w * electrons, electrons), electrons)
                for h in range(halves):
                    totals[h, place, :] = sums[u][:, h * 128 : (h + 1) * 128]

        def turn(d, carry):
            for e in range(elec):
                for h in range(halves):
                    low = e * orbitals + h * 128
                    nw_send[q, d, :, low : low + 128] = totals[
                        h, pl.ds(d * elec + e, width, stride=electrons), :
                    ].astype(jnp.bfloat16)
            return carry

        lax.fori_loop(0, blocks, turn, 0)
        exchange(me, blocks, nw_send, nw_recv, q, send_sems.at[2], recv_sems.at[2])

    def bias(q):
        left = nw_recv[q].reshape(blocks * width, elec * orbitals)
        step = min(256, nchol)

        @pl.loop(0, nchol // step)
        def _(n):
            at = pl.ds(pl.multiple_of(n * step, step), step)
            part = lax.dot_general(
                left, rotated[at, :], (((1,), (1,)), ((), ())), preferred_element_type=jnp.float32
            )
            fb_send[q, :, :, at] = part.astype(jnp.bfloat16).reshape(blocks, width, step)

        exchange(me, blocks, fb_send, fb_recv, q, send_sems.at[3], recv_sems.at[3])

    def finish(q):
        force_bias[q * width : (q + 1) * width, :] = lax.fori_loop(
            1,
            blocks,
            lambda s, acc: acc + fb_recv[q, s].astype(jnp.float32),
            fb_recv[q, 0].astype(jnp.float32),
        )

    for q in range(min(2, chunks)):
        send_operators(q)
    arrived(blocks, br_recv, 0, recv_sems.at[0])
    for q in range(chunks + 2):
        if q < chunks:
            arrived(blocks, op_recv, q, recv_sems.at[1])
            if q + 2 < chunks:
                send_operators(q + 2)
            taylor(q)
        if 1 <= q <= chunks:
            arrived(blocks, nw_recv, q - 1, recv_sems.at[2])
            bias(q - 1)
        if q >= 2:
            arrived(blocks, fb_recv, q - 2, recv_sems.at[3])
            finish(q - 2)
    arrived(blocks, br_send, 0, send_sems.at[0])
    for q in range(chunks):
        arrived(blocks, op_send, q, send_sems.at[1])
        arrived(blocks, nw_send, q, send_sems.at[2])
        arrived(blocks, fb_send, q, send_sems.at[3])


def shards(blocks, walkers, fields, chol_vectors, rotated, send_walker, slot_row):
    slots, electrons, orbitals = walkers.shape
    nchol, rows, _ = chol_vectors.shape
    elec = rotated.shape[1]
    cap = send_walker.shape[-1]
    width = min(chunk_slots, slots)
    chunks = slots // width
    gathered = lax.all_gather(fields, "chol", axis=0, tiled=False)
    gathered = gathered.reshape(blocks, chunks, width, nchol).swapaxes(0, 1)
    dims = (blocks, chunks, width, cap, rows, elec)
    bf16, f32 = jnp.bfloat16, jnp.float32
    vmem, smem = (pl.BlockSpec(memory_space=m) for m in (pltpu.VMEM, pltpu.SMEM))
    return pl.pallas_call(
        functools.partial(kernel, dims),
        out_shape=(
            jax.ShapeDtypeStruct(walkers.shape, bf16),
            jax.ShapeDtypeStruct((slots, nchol), f32),
        ),
        in_specs=[smem, smem, vmem, vmem, vmem, vmem],
        out_specs=(vmem, vmem),
        scratch_shapes=[
            pltpu.VMEM((1, blocks, cap, electrons, orbitals), bf16),
            pltpu.VMEM((1, blocks, cap, electrons, orbitals), bf16),
            pltpu.VMEM((chunks, blocks, width, rows * orbitals), bf16),
            pltpu.VMEM((chunks, blocks, width, rows * orbitals), bf16),
            pltpu.VMEM((orbitals // 128, width * orbitals, 128), f32),
            pltpu.VMEM((orbitals // 128, width * electrons, 128), f32),
            pltpu.VMEM((chunks, blocks, width, elec * orbitals), bf16),
            pltpu.VMEM((chunks, blocks, width, elec * orbitals), bf16),
            pltpu.VMEM((chunks, blocks, width, nchol), bf16),
            pltpu.VMEM((chunks, blocks, width, nchol), bf16),
            pltpu.SemaphoreType.DMA((4, chunks)),
            pltpu.SemaphoreType.DMA((4, chunks)),
        ],
        compiler_params=pltpu.CompilerParams(
            collective_id=0, has_side_effects=True, vmem_limit_bytes=60 * 1024 * 1024
        ),
    )(
        send_walker.reshape(-1),
        slot_row,
        walkers,
        gathered.reshape(chunks * blocks * width, nchol),
        chol_vectors.reshape(nchol, rows * orbitals),
        rotated.reshape(nchol, elec * orbitals),
    )


def solution(mesh):
    in_specs = (
        P(("grp", "chol"), None, None),
        P(("grp", "chol"), None),
        P(None, "chol", None),
        P(None, "chol", None),
        P(("grp", "chol"), None, None),
        P(("grp", "chol")),
    )
    out_specs = (P(("grp", "chol"), None, None), P(("grp", "chol"), None))
    return jax.shard_map(
        functools.partial(shards, mesh.shape["chol"]),
        mesh=mesh,
        in_specs=in_specs,
        out_specs=out_specs,
        check_vma=False,
    )
```

```python
import functools
import math

import jax
import jax.numpy as jnp
from jax import lax
from jax.experimental import pallas as pl
from jax.experimental.pallas import tpu as pltpu
from jax.sharding import PartitionSpec as P

field_scale = 1.5
chunk_slots = 16
degrees = 5
unfold_depth = 64
MESH = pl.DeviceIdType.MESH


def unfold(source, scratch, target):
    depth, rows, orbitals = source.shape
    step = scratch.shape[1] // rows

    def body(b, carry):
        first = pl.multiple_of(b * step, step)
        block = source[pl.ds(first, step)].astype(jnp.float32).reshape(step * rows, orbitals)
        for h in range(orbitals // 128):
            scratch[h] = block[:, h * 128 : (h + 1) * 128]
        for r in range(rows):
            for h in range(orbitals // 128):
                low = r * orbitals + h * 128
                target[pl.ds(first, step), low : low + 128] = scratch[
                    h, pl.ds(r, step, stride=rows), :
                ].astype(jnp.bfloat16)
        return carry

    lax.fori_loop(0, depth // step, body, 0)


def exchange(me, blocks, send, recv, chunk, send_sem, recv_sem, place=lambda d: d):
    def step(k, carry):
        peer = lax.rem(me + k, blocks)
        pltpu.make_async_remote_copy(
            src_ref=send.at[chunk, place(peer)],
            dst_ref=recv.at[chunk, me],
            send_sem=send_sem.at[chunk],
            recv_sem=recv_sem.at[chunk],
            device_id={"chol": peer},
            device_id_type=MESH,
        ).start()
        return carry

    lax.fori_loop(1, blocks, step, 0)
    recv[chunk, me] = send[chunk, place(me)]


def arrived(blocks, recv, chunk, sem):
    whole = recv.at[chunk, pl.ds(0, blocks - 1)]
    pltpu.make_async_copy(whole, whole, sem.at[chunk]).wait()


def kernel(
    dims,
    send_walker,
    slot_row,
    walkers,
    fields,
    chol_hbm,
    rotated_raw,
    new_walkers,
    force_bias,
    chol_raw,
    chol_wide,
    chol,
    rotated_wide,
    rotated,
    all_fields,
    br_send,
    br_recv,
    op_send,
    op_recv,
    op_rows,
    totals,
    nw_send,
    nw_recv,
    fb_send,
    fb_recv,
    send_sems,
    recv_sems,
    field_sems,
    load_sem,
):
    blocks, chunks, width, cap, rows, elec = dims
    slots, electrons, orbitals = walkers.shape
    nchol = rotated.shape[0]
    halves = orbitals // 128
    me = lax.axis_index("chol")
    pairs = blocks // 2
    core, pair = lax.rem(me, 2), me // 2
    load = pltpu.make_async_copy(chol_hbm, chol_raw, load_sem)
    load.start()

    barrier = pltpu.get_barrier_semaphore()

    def greet(k, carry):
        pl.semaphore_signal(
            barrier, inc=1, device_id={"chol": lax.rem(me + k, blocks)}, device_id_type=MESH
        )
        return carry

    lax.fori_loop(1, blocks, greet, 0)

    def pick(d, carry):
        for c in range(cap):
            br_send[0, d, c] = walkers[jnp.maximum(send_walker[d * cap + c], 0)]
        return carry

    lax.fori_loop(0, blocks, pick, 0)
    pl.semaphore_wait(barrier, blocks - 1)

    def share(k, carry):
        pltpu.make_async_remote_copy(
            src_ref=fields,
            dst_ref=all_fields.at[core, pair],
            send_sem=field_sems.at[0],
            recv_sem=field_sems.at[1],
            device_id={"chol": lax.rem(pair + k, pairs) * 2 + core},
            device_id_type=MESH,
        ).start()
        return carry

    lax.fori_loop(1, pairs, share, 0)
    all_fields[core, pair] = fields[...]
    load.wait()
    unfold(chol_raw, chol_wide, chol)
    same_core = all_fields.at[core, pl.ds(0, pairs - 1)]
    pltpu.make_async_copy(same_core, same_core, field_sems.at[1]).wait()
    across = pltpu.make_async_remote_copy(
        src_ref=all_fields.at[core],
        dst_ref=all_fields.at[core],
        send_sem=field_sems.at[2],
        recv_sem=field_sems.at[3],
        device_id={"chol": pair * 2 + 1 - core},
        device_id_type=MESH,
    )
    across.start()
    exchange(me, blocks, br_send, br_recv, 0, send_sems.at[0], recv_sems.at[0])

    across.wait_recv()
    scale = field_scale / math.sqrt(nchol)
    cols = rows * orbitals
    tile = min(512, cols)

    @pl.loop(0, cols // tile)
    def _(n):
        at = pl.ds(pl.multiple_of(n * tile, tile), tile)
        left = all_fields[...].reshape(blocks * slots, nchol)
        part = jnp.dot(left, chol[:, at], preferred_element_type=jnp.float32) * scale
        part = part.astype(jnp.bfloat16).reshape(blocks, chunks, width, tile)
        for q in range(chunks):
            op_send[q, :, :, at] = part[:, q]

    def send_operators(q):
        exchange(me, blocks, op_send, op_recv, q, send_sems.at[1], recv_sems.at[1], place)

    def place(d):
        return lax.rem(d, 2) * pairs + d // 2

    def taylor(q):
        def spread(s, carry):
            block = op_recv[q, s].astype(jnp.float32)
            for r in range(rows):
                for h in range(halves):
                    low = r * orbitals + h * 128
                    op_rows[h, pl.ds(s * rows + r, width, stride=orbitals), :] = block[
                        :, low : low + 128
                    ]
            return carry

        lax.fori_loop(0, blocks, spread, 0)
        group = 4

        @pl.loop(0, width // group)
        def _(g):
            ops, terms, sums = [], [], []
            for u in range(group):
                w = g * group + u
                first = pl.ds(pl.multiple_of(w * orbitals, orbitals), orbitals)
                ops.append(
                    jnp.concatenate([op_rows[h, first, :] for h in range(halves)], axis=1).astype(
                        jnp.bfloat16
                    )
                )
                row = slot_row[q * width + w]
                terms.append(br_recv[0, row // cap, row % cap])
                sums.append(terms[u].astype(jnp.float32))
            for degree in range(1, degrees + 1):
                for u in range(group):
                    product = lax.dot_general(
                        terms[u],
                        ops[u],
                        (((1,), (1,)), ((), ())),
                        preferred_element_type=jnp.float32,
                    )
                    terms[u] = (product * (1.0 / degree)).astype(jnp.bfloat16)
                    sums[u] = sums[u] + terms[u].astype(jnp.float32)
            for u in range(group):
                w = g * group + u
                new_walkers[q * width + w] = sums[u].astype(jnp.bfloat16)
                place = pl.ds(pl.multiple_of(w * electrons, electrons), electrons)
                for h in range(halves):
                    totals[h, place, :] = sums[u][:, h * 128 : (h + 1) * 128]

        def turn(d, carry):
            for e in range(elec):
                for h in range(halves):
                    low = e * orbitals + h * 128
                    nw_send[q, d, :, low : low + 128] = totals[
                        h, pl.ds(d * elec + e, width, stride=electrons), :
                    ].astype(jnp.bfloat16)
            return carry

        lax.fori_loop(0, blocks, turn, 0)
        exchange(me, blocks, nw_send, nw_recv, q, send_sems.at[2], recv_sems.at[2])

    def bias(q):
        left = nw_recv[q].reshape(blocks * width, elec * orbitals)
        step = min(256, nchol)

        @pl.loop(0, nchol // step)
        def _(n):
            at = pl.ds(pl.multiple_of(n * step, step), step)
            part = lax.dot_general(
                left, rotated[at, :], (((1,), (1,)), ((), ())), preferred_element_type=jnp.float32
            )
            fb_send[q, :, :, at] = part.astype(jnp.bfloat16).reshape(blocks, width, step)

        exchange(me, blocks, fb_send, fb_recv, q, send_sems.at[3], recv_sems.at[3])

    def finish(q):
        force_bias[q * width : (q + 1) * width, :] = lax.fori_loop(
            1,
            blocks,
            lambda s, acc: acc + fb_recv[q, s].astype(jnp.float32),
            fb_recv[q, 0].astype(jnp.float32),
        )

    for q in range(min(2, chunks)):
        send_operators(q)
    unfold(rotated_raw, rotated_wide, rotated)
    arrived(blocks, br_recv, 0, recv_sems.at[0])
    for q in range(chunks + 2):
        if q < chunks:
            arrived(blocks, op_recv, q, recv_sems.at[1])
            if q + 2 < chunks:
                send_operators(q + 2)
            taylor(q)
        if 1 <= q <= chunks:
            arrived(blocks, nw_recv, q - 1, recv_sems.at[2])
            bias(q - 1)
        if q >= 2:
            arrived(blocks, fb_recv, q - 2, recv_sems.at[3])
            finish(q - 2)
    arrived(blocks, br_send, 0, send_sems.at[0])
    across.wait_send()
    pltpu.make_async_copy(same_core, same_core, field_sems.at[0]).wait()
    for q in range(chunks):
        arrived(blocks, op_send, q, send_sems.at[1])
        arrived(blocks, nw_send, q, send_sems.at[2])
        arrived(blocks, fb_send, q, send_sems.at[3])


def shards(blocks, walkers, fields, chol_vectors, rotated, send_walker, slot_row):
    slots, electrons, orbitals = walkers.shape
    nchol, rows, _ = chol_vectors.shape
    elec = rotated.shape[1]
    cap = send_walker.shape[-1]
    width = min(chunk_slots, slots)
    chunks = slots // width
    dims = (blocks, chunks, width, cap, rows, elec)
    bf16, f32 = jnp.bfloat16, jnp.float32
    vmem, smem = (pl.BlockSpec(memory_space=m) for m in (pltpu.VMEM, pltpu.SMEM))
    return pl.pallas_call(
        functools.partial(kernel, dims),
        out_shape=(
            jax.ShapeDtypeStruct(walkers.shape, bf16),
            jax.ShapeDtypeStruct((slots, nchol), f32),
        ),
        in_specs=[smem, smem, vmem, vmem, pl.BlockSpec(memory_space=pl.ANY), vmem],
        out_specs=(vmem, vmem),
        scratch_shapes=[
            pltpu.VMEM(chol_vectors.shape, bf16),
            pltpu.VMEM((orbitals // 128, rows * unfold_depth, 128), f32),
            pltpu.VMEM((nchol, rows * orbitals), bf16),
            pltpu.VMEM((orbitals // 128, elec * unfold_depth, 128), f32),
            pltpu.VMEM((nchol, elec * orbitals), bf16),
            pltpu.VMEM((2, blocks // 2, slots, nchol), bf16),
            pltpu.VMEM((1, blocks, cap, electrons, orbitals), bf16),
            pltpu.VMEM((1, blocks, cap, electrons, orbitals), bf16),
            pltpu.VMEM((chunks, blocks, width, rows * orbitals), bf16),
            pltpu.VMEM((chunks, blocks, width, rows * orbitals), bf16),
            pltpu.VMEM((orbitals // 128, width * orbitals, 128), f32),
            pltpu.VMEM((orbitals // 128, width * electrons, 128), f32),
            pltpu.VMEM((chunks, blocks, width, elec * orbitals), bf16),
            pltpu.VMEM((chunks, blocks, width, elec * orbitals), bf16),
            pltpu.VMEM((chunks, blocks, width, nchol), bf16),
            pltpu.VMEM((chunks, blocks, width, nchol), bf16),
            pltpu.SemaphoreType.DMA((4, chunks)),
            pltpu.SemaphoreType.DMA((4, chunks)),
            pltpu.SemaphoreType.DMA((4,)),
            pltpu.SemaphoreType.DMA,
        ],
        compiler_params=pltpu.CompilerParams(
            collective_id=0, has_side_effects=True, vmem_limit_bytes=60 * 1024 * 1024
        ),
    )(
        send_walker.reshape(-1),
        slot_row,
        walkers,
        fields,
        chol_vectors,
        rotated,
    )


def solution(mesh):
    in_specs = (
        P(("grp", "chol"), None, None),
        P(("grp", "chol"), None),
        P(None, "chol", None),
        P(None, "chol", None),
        P(("grp", "chol"), None, None),
        P(("grp", "chol")),
    )
    out_specs = (P(("grp", "chol"), None, None), P(("grp", "chol"), None))
    return jax.shard_map(
        functools.partial(shards, mesh.shape["chol"]),
        mesh=mesh,
        in_specs=in_specs,
        out_specs=out_specs,
        check_vma=False,
    )
```

```python
import functools
import math

import jax
import jax.numpy as jnp
from jax import lax
from jax.experimental import pallas as pl
from jax.experimental.pallas import tpu as pltpu
from jax.sharding import PartitionSpec as P

field_scale = 1.5
chunk_slots = 8
degrees = 5
unfold_depth = 64
MESH = pl.DeviceIdType.MESH


def unfold(source, scratch, target):
    depth, rows, orbitals = source.shape
    step = scratch.shape[1] // rows

    def body(b, carry):
        first = pl.multiple_of(b * step, step)
        block = source[pl.ds(first, step)].astype(jnp.float32).reshape(step * rows, orbitals)
        for h in range(orbitals // 128):
            scratch[h] = block[:, h * 128 : (h + 1) * 128]
        for r in range(rows):
            for h in range(orbitals // 128):
                low = r * orbitals + h * 128
                target[pl.ds(first, step), low : low + 128] = scratch[
                    h, pl.ds(r, step, stride=rows), :
                ].astype(jnp.bfloat16)
        return carry

    lax.fori_loop(0, depth // step, body, 0)


def exchange(me, blocks, send, recv, chunk, send_sem, recv_sem, place=lambda d: d):
    def step(k, carry):
        peer = lax.rem(me + k, blocks)
        pltpu.make_async_remote_copy(
            src_ref=send.at[chunk, place(peer)],
            dst_ref=recv.at[chunk, me],
            send_sem=send_sem.at[chunk],
            recv_sem=recv_sem.at[chunk],
            device_id={"chol": peer},
            device_id_type=MESH,
        ).start()
        return carry

    lax.fori_loop(1, blocks, step, 0)
    recv[chunk, me] = send[chunk, place(me)]


def arrived(blocks, recv, chunk, sem):
    whole = recv.at[chunk, pl.ds(0, blocks - 1)]
    pltpu.make_async_copy(whole, whole, sem.at[chunk]).wait()


def kernel(
    dims,
    send_walker,
    slot_row,
    walkers,
    fields,
    chol_hbm,
    rotated_raw,
    new_walkers,
    force_bias,
    chol_raw,
    chol_wide,
    chol,
    rotated_wide,
    rotated,
    all_fields,
    br_send,
    br_recv,
    op_send,
    op_recv,
    op_rows,
    totals,
    nw_send,
    nw_recv,
    fb_send,
    fb_recv,
    send_sems,
    recv_sems,
    field_sems,
    load_sem,
):
    blocks, chunks, width, cap, rows, elec = dims
    slots, electrons, orbitals = walkers.shape
    nchol = rotated.shape[0]
    halves = orbitals // 128
    me = lax.axis_index("chol")
    pairs = blocks // 2
    core, pair = lax.rem(me, 2), me // 2
    load = pltpu.make_async_copy(chol_hbm, chol_raw, load_sem)
    load.start()

    barrier = pltpu.get_barrier_semaphore()

    def greet(k, carry):
        pl.semaphore_signal(
            barrier, inc=1, device_id={"chol": lax.rem(me + k, blocks)}, device_id_type=MESH
        )
        return carry

    lax.fori_loop(1, blocks, greet, 0)

    def pick(d, carry):
        for c in range(cap):
            br_send[0, d, c] = walkers[jnp.maximum(send_walker[d * cap + c], 0)]
        return carry

    lax.fori_loop(0, blocks, pick, 0)
    pl.semaphore_wait(barrier, blocks - 1)

    def share(k, carry):
        pltpu.make_async_remote_copy(
            src_ref=fields,
            dst_ref=all_fields.at[core, pair],
            send_sem=field_sems.at[0],
            recv_sem=field_sems.at[1],
            device_id={"chol": lax.rem(pair + k, pairs) * 2 + core},
            device_id_type=MESH,
        ).start()
        return carry

    lax.fori_loop(1, pairs, share, 0)
    all_fields[core, pair] = fields[...]
    load.wait()
    unfold(chol_raw, chol_wide, chol)
    same_core = all_fields.at[core, pl.ds(0, pairs - 1)]
    pltpu.make_async_copy(same_core, same_core, field_sems.at[1]).wait()
    across = pltpu.make_async_remote_copy(
        src_ref=all_fields.at[core],
        dst_ref=all_fields.at[core],
        send_sem=field_sems.at[2],
        recv_sem=field_sems.at[3],
        device_id={"chol": pair * 2 + 1 - core},
        device_id_type=MESH,
    )
    across.start()
    exchange(me, blocks, br_send, br_recv, 0, send_sems.at[0], recv_sems.at[0])

    across.wait_recv()
    scale = field_scale / math.sqrt(nchol)
    cols = rows * orbitals
    tile = min(512, cols)

    @pl.loop(0, cols // tile)
    def _(n):
        at = pl.ds(pl.multiple_of(n * tile, tile), tile)
        left = all_fields[...].reshape(blocks * slots, nchol)
        part = jnp.dot(left, chol[:, at], preferred_element_type=jnp.float32) * scale
        part = part.astype(jnp.bfloat16).reshape(blocks, chunks, width, tile)
        for q in range(chunks):
            op_send[q, :, :, at] = part[:, q]

    def send_operators(q):
        exchange(me, blocks, op_send, op_recv, q, send_sems.at[1], recv_sems.at[1], place)

    def place(d):
        return lax.rem(d, 2) * pairs + d // 2

    def taylor(q):
        def spread(s, carry):
            block = op_recv[q, s].astype(jnp.float32)
            for r in range(rows):
                for h in range(halves):
                    low = r * orbitals + h * 128
                    op_rows[h, pl.ds(s * rows + r, width, stride=orbitals), :] = block[
                        :, low : low + 128
                    ]
            return carry

        lax.fori_loop(0, blocks, spread, 0)
        group = 4

        @pl.loop(0, width // group)
        def _(g):
            ops, terms, sums = [], [], []
            for u in range(group):
                w = g * group + u
                first = pl.ds(pl.multiple_of(w * orbitals, orbitals), orbitals)
                ops.append(
                    jnp.concatenate([op_rows[h, first, :] for h in range(halves)], axis=1).astype(
                        jnp.bfloat16
                    )
                )
                row = slot_row[q * width + w]
                terms.append(br_recv[0, row // cap, row % cap])
                sums.append(terms[u].astype(jnp.float32))
            for degree in range(1, degrees + 1):
                for u in range(group):
                    product = lax.dot_general(
                        terms[u],
                        ops[u],
                        (((1,), (1,)), ((), ())),
                        preferred_element_type=jnp.float32,
                    )
                    terms[u] = (product * (1.0 / degree)).astype(jnp.bfloat16)
                    sums[u] = sums[u] + terms[u].astype(jnp.float32)
            for u in range(group):
                w = g * group + u
                new_walkers[q * width + w] = sums[u].astype(jnp.bfloat16)
                place = pl.ds(pl.multiple_of(w * electrons, electrons), electrons)
                for h in range(halves):
                    totals[h, place, :] = sums[u][:, h * 128 : (h + 1) * 128]

        def turn(d, carry):
            for e in range(elec):
                for h in range(halves):
                    low = e * orbitals + h * 128
                    nw_send[q, d, :, low : low + 128] = totals[
                        h, pl.ds(d * elec + e, width, stride=electrons), :
                    ].astype(jnp.bfloat16)
            return carry

        lax.fori_loop(0, blocks, turn, 0)
        exchange(me, blocks, nw_send, nw_recv, q, send_sems.at[2], recv_sems.at[2])

    def bias(q):
        left = nw_recv[q].reshape(blocks * width, elec * orbitals)
        step = min(256, nchol)

        @pl.loop(0, nchol // step)
        def _(n):
            at = pl.ds(pl.multiple_of(n * step, step), step)
            part = lax.dot_general(
                left, rotated[at, :], (((1,), (1,)), ((), ())), preferred_element_type=jnp.float32
            )
            fb_send[q, :, :, at] = part.astype(jnp.bfloat16).reshape(blocks, width, step)

        exchange(me, blocks, fb_send, fb_recv, q, send_sems.at[3], recv_sems.at[3])

    def finish(q):
        force_bias[q * width : (q + 1) * width, :] = lax.fori_loop(
            1,
            blocks,
            lambda s, acc: acc + fb_recv[q, s].astype(jnp.float32),
            fb_recv[q, 0].astype(jnp.float32),
        )

    for q in range(min(2, chunks)):
        send_operators(q)
    unfold(rotated_raw, rotated_wide, rotated)
    arrived(blocks, br_recv, 0, recv_sems.at[0])
    for q in range(chunks + 2):
        if q < chunks:
            arrived(blocks, op_recv, q, recv_sems.at[1])
            if q + 2 < chunks:
                send_operators(q + 2)
            taylor(q)
        if 1 <= q <= chunks:
            arrived(blocks, nw_recv, q - 1, recv_sems.at[2])
            bias(q - 1)
        if q >= 2:
            arrived(blocks, fb_recv, q - 2, recv_sems.at[3])
            finish(q - 2)
    arrived(blocks, br_send, 0, send_sems.at[0])
    across.wait_send()
    pltpu.make_async_copy(same_core, same_core, field_sems.at[0]).wait()
    for q in range(chunks):
        arrived(blocks, op_send, q, send_sems.at[1])
        arrived(blocks, nw_send, q, send_sems.at[2])
        arrived(blocks, fb_send, q, send_sems.at[3])


def shards(blocks, walkers, fields, chol_vectors, rotated, send_walker, slot_row):
    slots, electrons, orbitals = walkers.shape
    nchol, rows, _ = chol_vectors.shape
    elec = rotated.shape[1]
    cap = send_walker.shape[-1]
    width = min(chunk_slots, slots)
    chunks = slots // width
    dims = (blocks, chunks, width, cap, rows, elec)
    bf16, f32 = jnp.bfloat16, jnp.float32
    vmem, smem = (pl.BlockSpec(memory_space=m) for m in (pltpu.VMEM, pltpu.SMEM))
    return pl.pallas_call(
        functools.partial(kernel, dims),
        out_shape=(
            jax.ShapeDtypeStruct(walkers.shape, bf16),
            jax.ShapeDtypeStruct((slots, nchol), f32),
        ),
        in_specs=[smem, smem, vmem, vmem, pl.BlockSpec(memory_space=pl.ANY), vmem],
        out_specs=(vmem, vmem),
        scratch_shapes=[
            pltpu.VMEM(chol_vectors.shape, bf16),
            pltpu.VMEM((orbitals // 128, rows * unfold_depth, 128), f32),
            pltpu.VMEM((nchol, rows * orbitals), bf16),
            pltpu.VMEM((orbitals // 128, elec * unfold_depth, 128), f32),
            pltpu.VMEM((nchol, elec * orbitals), bf16),
            pltpu.VMEM((2, blocks // 2, slots, nchol), bf16),
            pltpu.VMEM((1, blocks, cap, electrons, orbitals), bf16),
            pltpu.VMEM((1, blocks, cap, electrons, orbitals), bf16),
            pltpu.VMEM((chunks, blocks, width, rows * orbitals), bf16),
            pltpu.VMEM((chunks, blocks, width, rows * orbitals), bf16),
            pltpu.VMEM((orbitals // 128, width * orbitals, 128), f32),
            pltpu.VMEM((orbitals // 128, width * electrons, 128), f32),
            pltpu.VMEM((chunks, blocks, width, elec * orbitals), bf16),
            pltpu.VMEM((chunks, blocks, width, elec * orbitals), bf16),
            pltpu.VMEM((chunks, blocks, width, nchol), bf16),
            pltpu.VMEM((chunks, blocks, width, nchol), bf16),
            pltpu.SemaphoreType.DMA((4, chunks)),
            pltpu.SemaphoreType.DMA((4, chunks)),
            pltpu.SemaphoreType.DMA((4,)),
            pltpu.SemaphoreType.DMA,
        ],
        compiler_params=pltpu.CompilerParams(
            collective_id=0, has_side_effects=True, vmem_limit_bytes=60 * 1024 * 1024
        ),
    )(
        send_walker.reshape(-1),
        slot_row,
        walkers,
        fields,
        chol_vectors,
        rotated,
    )


def solution(mesh):
    in_specs = (
        P(("grp", "chol"), None, None),
        P(("grp", "chol"), None),
        P(None, "chol", None),
        P(None, "chol", None),
        P(("grp", "chol"), None, None),
        P(("grp", "chol")),
    )
    out_specs = (P(("grp", "chol"), None, None), P(("grp", "chol"), None))
    return jax.shard_map(
        functools.partial(shards, mesh.shape["chol"]),
        mesh=mesh,
        in_specs=in_specs,
        out_specs=out_specs,
        check_vma=False,
    )
```

```python
import functools
import math

import jax
import jax.numpy as jnp
from jax import lax
from jax.experimental import pallas as pl
from jax.experimental.pallas import tpu as pltpu
from jax.sharding import PartitionSpec as P

field_scale = 1.5
chunk_slots = 16
degrees = 5
unfold_depth = 64
MESH = pl.DeviceIdType.MESH


def unfold(source, scratch, target):
    depth, rows, orbitals = source.shape
    step = scratch.shape[1] // rows

    def body(b, carry):
        first = pl.multiple_of(b * step, step)
        block = source[pl.ds(first, step)].astype(jnp.float32).reshape(step * rows, orbitals)
        for h in range(orbitals // 128):
            scratch[h] = block[:, h * 128 : (h + 1) * 128]
        for r in range(rows):
            for h in range(orbitals // 128):
                low = r * orbitals + h * 128
                target[pl.ds(first, step), low : low + 128] = scratch[
                    h, pl.ds(r, step, stride=rows), :
                ].astype(jnp.bfloat16)
        return carry

    lax.fori_loop(0, depth // step, body, 0)


def exchange(me, blocks, send, recv, chunk, send_sem, recv_sem, place=lambda d: d, land=lambda d: d):
    hop = next(h for h in (7, 5, 3, 1) if math.gcd(h, blocks) == 1)

    def step(k, carry):
        peer = lax.rem(me + k * hop, blocks)
        pltpu.make_async_remote_copy(
            src_ref=send.at[chunk, place(peer)],
            dst_ref=recv.at[chunk, land(me)],
            send_sem=send_sem.at[chunk],
            recv_sem=recv_sem.at[chunk],
            device_id={"chol": peer},
            device_id_type=MESH,
        ).start()
        return carry

    lax.fori_loop(1, blocks, step, 0)
    recv[chunk, land(me)] = send[chunk, place(me)]


def arrived(blocks, recv, chunk, sem):
    whole = recv.at[chunk, pl.ds(0, blocks - 1)]
    pltpu.make_async_copy(whole, whole, sem.at[chunk]).wait()


def kernel(
    dims,
    send_walker,
    slot_row,
    walkers,
    fields,
    chol_hbm,
    rotated_raw,
    new_walkers,
    force_bias,
    chol_raw,
    chol_wide,
    chol,
    rotated_wide,
    rotated,
    all_fields,
    br_send,
    br_recv,
    op_send,
    op_recv,
    op_rows,
    totals,
    nw_send,
    nw_recv,
    pair_send,
    pair_recv,
    pair_own,
    fb_send,
    fb_recv,
    send_sems,
    recv_sems,
    field_sems,
    load_sem,
):
    blocks, chunks, width, cap, rows, elec = dims
    slots, electrons, orbitals = walkers.shape
    nchol = rotated.shape[0]
    halves = orbitals // 128
    me = lax.axis_index("chol")
    pairs = blocks // 2
    core, pair = lax.rem(me, 2), me // 2
    load = pltpu.make_async_copy(chol_hbm, chol_raw, load_sem)
    load.start()

    barrier = pltpu.get_barrier_semaphore()

    def greet(k, carry):
        pl.semaphore_signal(
            barrier, inc=1, device_id={"chol": lax.rem(me + k, blocks)}, device_id_type=MESH
        )
        return carry

    lax.fori_loop(1, blocks, greet, 0)

    def pick(d, carry):
        for c in range(cap):
            br_send[0, d, c] = walkers[jnp.maximum(send_walker[d * cap + c], 0)]
        return carry

    lax.fori_loop(0, blocks, pick, 0)
    pl.semaphore_wait(barrier, blocks - 1)

    def share(k, carry):
        pltpu.make_async_remote_copy(
            src_ref=fields,
            dst_ref=all_fields.at[core, pair],
            send_sem=field_sems.at[0],
            recv_sem=field_sems.at[1],
            device_id={"chol": lax.rem(pair + k, pairs) * 2 + core},
            device_id_type=MESH,
        ).start()
        return carry

    lax.fori_loop(1, pairs, share, 0)
    all_fields[core, pair] = fields[...]
    load.wait()
    unfold(chol_raw, chol_wide, chol)
    same_core = all_fields.at[core, pl.ds(0, pairs - 1)]
    pltpu.make_async_copy(same_core, same_core, field_sems.at[1]).wait()
    across = pltpu.make_async_remote_copy(
        src_ref=all_fields.at[core],
        dst_ref=all_fields.at[core],
        send_sem=field_sems.at[2],
        recv_sem=field_sems.at[3],
        device_id={"chol": pair * 2 + 1 - core},
        device_id_type=MESH,
    )
    across.start()
    exchange(me, blocks, br_send, br_recv, 0, send_sems.at[0], recv_sems.at[0])

    across.wait_recv()
    scale = field_scale / math.sqrt(nchol)
    cols = rows * orbitals
    tile = min(512, cols)

    @pl.loop(0, cols // tile)
    def _(n):
        at = pl.ds(pl.multiple_of(n * tile, tile), tile)
        left = all_fields[...].reshape(blocks * slots, nchol)
        part = jnp.dot(left, chol[:, at], preferred_element_type=jnp.float32) * scale
        part = part.astype(jnp.bfloat16).reshape(blocks, chunks, width, tile)
        for q in range(chunks):
            op_send[q, :, :, at] = part[:, q]

    def send_operators(q):
        exchange(me, blocks, op_send, op_recv, q, send_sems.at[1], recv_sems.at[1], place)

    def place(d):
        return lax.rem(d, 2) * pairs + d // 2

    def taylor(q):
        def spread(s, carry):
            block = op_recv[q, s].astype(jnp.float32)
            for r in range(rows):
                for h in range(halves):
                    low = r * orbitals + h * 128
                    op_rows[h, pl.ds(s * rows + r, width, stride=orbitals), :] = block[
                        :, low : low + 128
                    ]
            return carry

        lax.fori_loop(0, blocks, spread, 0)
        group = 4

        @pl.loop(0, width // group)
        def _(g):
            ops, terms, sums = [], [], []
            for u in range(group):
                w = g * group + u
                first = pl.ds(pl.multiple_of(w * orbitals, orbitals), orbitals)
                ops.append(
                    jnp.concatenate([op_rows[h, first, :] for h in range(halves)], axis=1).astype(
                        jnp.bfloat16
                    )
                )
                row = slot_row[q * width + w]
                terms.append(br_recv[0, row // cap, row % cap])
                sums.append(terms[u].astype(jnp.float32))
            for degree in range(1, degrees + 1):
                for u in range(group):
                    product = lax.dot_general(
                        terms[u],
                        ops[u],
                        (((1,), (1,)), ((), ())),
                        preferred_element_type=jnp.float32,
                    )
                    terms[u] = (product * (1.0 / degree)).astype(jnp.bfloat16)
                    sums[u] = sums[u] + terms[u].astype(jnp.float32)
            for u in range(group):
                w = g * group + u
                new_walkers[q * width + w] = sums[u].astype(jnp.bfloat16)
                place = pl.ds(pl.multiple_of(w * electrons, electrons), electrons)
                for h in range(halves):
                    totals[h, place, :] = sums[u][:, h * 128 : (h + 1) * 128]

        def turn(d, carry):
            for e in range(elec):
                for h in range(halves):
                    low = e * orbitals + h * 128
                    nw_send[q, d, :, low : low + 128] = totals[
                        h, pl.ds(d * elec + e, width, stride=electrons), :
                    ].astype(jnp.bfloat16)
            return carry

        lax.fori_loop(0, blocks, turn, 0)
        exchange(me, blocks, nw_send, nw_recv, q, send_sems.at[2], recv_sems.at[2], land=place)

    def partial(q, half, target):
        left = nw_recv[q, pl.ds(half * pairs, pairs)].reshape(pairs * width, elec * orbitals)
        step = min(256, nchol)

        @pl.loop(0, nchol // step)
        def _(n):
            at = pl.ds(pl.multiple_of(n * step, step), step)
            target[:, at] = lax.dot_general(
                left, rotated[at, :], (((1,), (1,)), ((), ())), preferred_element_type=jnp.float32
            )

    def bias(q):
        partial(q, 1 - core, pair_send.at[q])
        across = pltpu.make_async_remote_copy(
            src_ref=pair_send.at[q],
            dst_ref=pair_recv.at[q],
            send_sem=send_sems.at[4, q],
            recv_sem=recv_sems.at[4, q],
            device_id={"chol": pair * 2 + 1 - core},
            device_id_type=MESH,
        )
        across.start()
        partial(q, core, pair_own)
        across.wait_recv()
        both = (pair_own[...] + pair_recv[q]).astype(jnp.bfloat16)
        fb_send[q] = both.reshape(pairs, width, nchol)

        def step(k, carry):
            peer = lax.rem(pair + k, pairs)
            pltpu.make_async_remote_copy(
                src_ref=fb_send.at[q, peer],
                dst_ref=fb_recv.at[q, pair],
                send_sem=send_sems.at[3, q],
                recv_sem=recv_sems.at[3, q],
                device_id={"chol": peer * 2 + core},
                device_id_type=MESH,
            ).start()
            return carry

        lax.fori_loop(1, pairs, step, 0)
        fb_recv[q, pair] = fb_send[q, pair]

    def finish(q):
        force_bias[q * width : (q + 1) * width, :] = lax.fori_loop(
            1,
            pairs,
            lambda s, acc: acc + fb_recv[q, s].astype(jnp.float32),
            fb_recv[q, 0].astype(jnp.float32),
        )

    for q in range(min(2, chunks)):
        send_operators(q)
    unfold(rotated_raw, rotated_wide, rotated)
    arrived(blocks, br_recv, 0, recv_sems.at[0])
    for q in range(chunks + 2):
        if q < chunks:
            arrived(blocks, op_recv, q, recv_sems.at[1])
            if q + 2 < chunks:
                send_operators(q + 2)
            taylor(q)
        if 1 <= q <= chunks:
            arrived(blocks, nw_recv, q - 1, recv_sems.at[2])
            bias(q - 1)
        if q >= 2:
            arrived(pairs, fb_recv, q - 2, recv_sems.at[3])
            finish(q - 2)
    arrived(blocks, br_send, 0, send_sems.at[0])
    across.wait_send()
    pltpu.make_async_copy(same_core, same_core, field_sems.at[0]).wait()
    for q in range(chunks):
        arrived(blocks, op_send, q, send_sems.at[1])
        arrived(blocks, nw_send, q, send_sems.at[2])
        arrived(pairs, fb_send, q, send_sems.at[3])
        pltpu.make_async_copy(pair_send.at[q], pair_send.at[q], send_sems.at[4, q]).wait()


def shards(blocks, walkers, fields, chol_vectors, rotated, send_walker, slot_row):
    slots, electrons, orbitals = walkers.shape
    nchol, rows, _ = chol_vectors.shape
    elec = rotated.shape[1]
    cap = send_walker.shape[-1]
    width = min(chunk_slots, slots)
    chunks = slots // width
    dims = (blocks, chunks, width, cap, rows, elec)
    bf16, f32 = jnp.bfloat16, jnp.float32
    vmem, smem = (pl.BlockSpec(memory_space=m) for m in (pltpu.VMEM, pltpu.SMEM))
    return pl.pallas_call(
        functools.partial(kernel, dims),
        out_shape=(
            jax.ShapeDtypeStruct(walkers.shape, bf16),
            jax.ShapeDtypeStruct((slots, nchol), f32),
        ),
        in_specs=[smem, smem, vmem, vmem, pl.BlockSpec(memory_space=pl.ANY), vmem],
        out_specs=(vmem, vmem),
        scratch_shapes=[
            pltpu.VMEM(chol_vectors.shape, bf16),
            pltpu.VMEM((orbitals // 128, rows * unfold_depth, 128), f32),
            pltpu.VMEM((nchol, rows * orbitals), bf16),
            pltpu.VMEM((orbitals // 128, elec * unfold_depth, 128), f32),
            pltpu.VMEM((nchol, elec * orbitals), bf16),
            pltpu.VMEM((2, blocks // 2, slots, nchol), bf16),
            pltpu.VMEM((1, blocks, cap, electrons, orbitals), bf16),
            pltpu.VMEM((1, blocks, cap, electrons, orbitals), bf16),
            pltpu.VMEM((chunks, blocks, width, rows * orbitals), bf16),
            pltpu.VMEM((chunks, blocks, width, rows * orbitals), bf16),
            pltpu.VMEM((orbitals // 128, width * orbitals, 128), f32),
            pltpu.VMEM((orbitals // 128, width * electrons, 128), f32),
            pltpu.VMEM((chunks, blocks, width, elec * orbitals), bf16),
            pltpu.VMEM((chunks, blocks, width, elec * orbitals), bf16),
            pltpu.VMEM((chunks, blocks // 2 * width, nchol), f32),
            pltpu.VMEM((chunks, blocks // 2 * width, nchol), f32),
            pltpu.VMEM((blocks // 2 * width, nchol), f32),
            pltpu.VMEM((chunks, blocks // 2, width, nchol), bf16),
            pltpu.VMEM((chunks, blocks // 2, width, nchol), bf16),
            pltpu.SemaphoreType.DMA((5, chunks)),
            pltpu.SemaphoreType.DMA((5, chunks)),
            pltpu.SemaphoreType.DMA((4,)),
            pltpu.SemaphoreType.DMA,
        ],
        compiler_params=pltpu.CompilerParams(
            collective_id=0, has_side_effects=True, vmem_limit_bytes=60 * 1024 * 1024
        ),
    )(
        send_walker.reshape(-1),
        slot_row,
        walkers,
        fields,
        chol_vectors,
        rotated,
    )


def solution(mesh):
    in_specs = (
        P(("grp", "chol"), None, None),
        P(("grp", "chol"), None),
        P(None, "chol", None),
        P(None, "chol", None),
        P(("grp", "chol"), None, None),
        P(("grp", "chol")),
    )
    out_specs = (P(("grp", "chol"), None, None), P(("grp", "chol"), None))
    return jax.shard_map(
        functools.partial(shards, mesh.shape["chol"]),
        mesh=mesh,
        in_specs=in_specs,
        out_specs=out_specs,
        check_vma=False,
    )
```

```python
import functools
import math

import jax
import jax.numpy as jnp
from jax import lax
from jax.experimental import pallas as pl
from jax.experimental.pallas import tpu as pltpu
from jax.sharding import PartitionSpec as P

field_scale = 1.5
chunk_slots = 16
degrees = 5
unfold_depth = 64
MESH = pl.DeviceIdType.MESH


def stride_of(blocks):
    return next(h for h in (7, 5, 3, 1) if math.gcd(h, blocks) == 1)


def unfold(source, scratch, target):
    depth, rows, orbitals = source.shape
    step = scratch.shape[1] // rows

    def body(b, carry):
        first = pl.multiple_of(b * step, step)
        block = source[pl.ds(first, step)].astype(jnp.float32).reshape(step * rows, orbitals)
        for h in range(orbitals // 128):
            scratch[h] = block[:, h * 128 : (h + 1) * 128]
        for r in range(rows):
            for h in range(orbitals // 128):
                low = r * orbitals + h * 128
                target[pl.ds(first, step), low : low + 128] = scratch[
                    h, pl.ds(r, step, stride=rows), :
                ].astype(jnp.bfloat16)
        return carry

    lax.fori_loop(0, depth // step, body, 0)


def exchange(me, blocks, send, recv, chunk, send_sem, recv_sem, place=lambda d: d, land=lambda d: d):
    hop = stride_of(blocks)

    def step(k, carry):
        peer = lax.rem(me + k * hop, blocks)
        pltpu.make_async_remote_copy(
            src_ref=send.at[chunk, place(peer)],
            dst_ref=recv.at[chunk, land(me)],
            send_sem=send_sem.at[chunk],
            recv_sem=recv_sem.at[chunk],
            device_id={"chol": peer},
            device_id_type=MESH,
        ).start()
        return carry

    lax.fori_loop(1, blocks, step, 0)
    recv[chunk, land(me)] = send[chunk, place(me)]


def arrived(blocks, recv, chunk, sem):
    whole = recv.at[chunk, pl.ds(0, blocks - 1)]
    pltpu.make_async_copy(whole, whole, sem.at[chunk]).wait()


def kernel(
    dims,
    send_walker,
    slot_row,
    walkers,
    fields,
    chol_hbm,
    rotated_raw,
    new_walkers,
    force_bias,
    chol_raw,
    chol_wide,
    chol,
    rotated_wide,
    rotated,
    all_fields,
    br_send,
    br_recv,
    op_send,
    op_recv,
    op_rows,
    totals,
    nw_send,
    nw_recv,
    pair_send,
    pair_recv,
    pair_own,
    fb_send,
    fb_recv,
    send_sems,
    recv_sems,
    field_sems,
    load_sem,
    op_sems,
):
    blocks, chunks, width, cap, rows, elec = dims
    slots, electrons, orbitals = walkers.shape
    nchol = rotated.shape[0]
    halves = orbitals // 128
    me = lax.axis_index("chol")
    pairs = blocks // 2
    core, pair = lax.rem(me, 2), me // 2
    groups = math.gcd(4, blocks)
    share_of = blocks // groups
    hop = stride_of(blocks)
    load = pltpu.make_async_copy(chol_hbm, chol_raw, load_sem)
    load.start()

    barrier = pltpu.get_barrier_semaphore()

    def greet(k, carry):
        pl.semaphore_signal(
            barrier, inc=1, device_id={"chol": lax.rem(me + k, blocks)}, device_id_type=MESH
        )
        return carry

    lax.fori_loop(1, blocks, greet, 0)

    def pick(d, carry):
        for c in range(cap):
            br_send[0, d, c] = walkers[jnp.maximum(send_walker[d * cap + c], 0)]
        return carry

    lax.fori_loop(0, blocks, pick, 0)
    pl.semaphore_wait(barrier, blocks - 1)

    def share(k, carry):
        pltpu.make_async_remote_copy(
            src_ref=fields,
            dst_ref=all_fields.at[core, pair],
            send_sem=field_sems.at[0],
            recv_sem=field_sems.at[1],
            device_id={"chol": lax.rem(pair + k, pairs) * 2 + core},
            device_id_type=MESH,
        ).start()
        return carry

    lax.fori_loop(1, pairs, share, 0)
    all_fields[core, pair] = fields[...]
    load.wait()
    unfold(chol_raw, chol_wide, chol)
    same_core = all_fields.at[core, pl.ds(0, pairs - 1)]
    pltpu.make_async_copy(same_core, same_core, field_sems.at[1]).wait()
    across = pltpu.make_async_remote_copy(
        src_ref=all_fields.at[core],
        dst_ref=all_fields.at[core],
        send_sem=field_sems.at[2],
        recv_sem=field_sems.at[3],
        device_id={"chol": pair * 2 + 1 - core},
        device_id_type=MESH,
    )
    across.start()
    exchange(me, blocks, br_send, br_recv, 0, send_sems.at[0], recv_sems.at[0])

    across.wait_recv()
    scale = field_scale / math.sqrt(nchol)
    cols = rows * orbitals
    tile = min(512, cols)

    @pl.loop(0, cols // tile)
    def _(n):
        at = pl.ds(pl.multiple_of(n * tile, tile), tile)
        left = all_fields[...].reshape(blocks * slots, nchol)
        part = jnp.dot(left, chol[:, at], preferred_element_type=jnp.float32) * scale
        part = part.astype(jnp.bfloat16).reshape(blocks, chunks, width, tile)
        for q in range(chunks):
            op_send[q, :, :, at] = part[:, q]

    def send_operators(q):
        for group in range(groups):
            def step(k, carry):
                peer = lax.rem(me + k * hop, blocks)
                pltpu.make_async_remote_copy(
                    src_ref=op_send.at[q, place(peer)],
                    dst_ref=op_recv.at[q, me],
                    send_sem=send_sems.at[1, q],
                    recv_sem=op_sems.at[q, group],
                    device_id={"chol": peer},
                    device_id_type=MESH,
                ).start()
                return carry

            lax.fori_loop(max(1, group * share_of), (group + 1) * share_of, step, 0)
        op_recv[q, me] = op_send[q, place(me)]

    def place(d):
        return lax.rem(d, 2) * pairs + d // 2

    def taylor(q):
        def spread(k, carry):
            s = lax.rem(me + (blocks - k) * hop, blocks)
            block = op_recv[q, s].astype(jnp.float32)
            for r in range(rows):
                for h in range(halves):
                    low = r * orbitals + h * 128
                    op_rows[h, pl.ds(s * rows + r, width, stride=orbitals), :] = block[
                        :, low : low + 128
                    ]
            return carry

        for group in range(groups):
            count = share_of - 1 if group == 0 else share_of
            whole = op_recv.at[q, pl.ds(0, count)]
            pltpu.make_async_copy(whole, whole, op_sems.at[q, group]).wait()
            lax.fori_loop(group * share_of, (group + 1) * share_of, spread, 0)
        group = 4

        @pl.loop(0, width // group)
        def _(g):
            ops, terms, sums = [], [], []
            for u in range(group):
                w = g * group + u
                first = pl.ds(pl.multiple_of(w * orbitals, orbitals), orbitals)
                ops.append(
                    jnp.concatenate([op_rows[h, first, :] for h in range(halves)], axis=1).astype(
                        jnp.bfloat16
                    )
                )
                row = slot_row[q * width + w]
                terms.append(br_recv[0, row // cap, row % cap])
                sums.append(terms[u].astype(jnp.float32))
            for degree in range(1, degrees + 1):
                for u in range(group):
                    product = lax.dot_general(
                        terms[u],
                        ops[u],
                        (((1,), (1,)), ((), ())),
                        preferred_element_type=jnp.float32,
                    )
                    terms[u] = (product * (1.0 / degree)).astype(jnp.bfloat16)
                    sums[u] = sums[u] + terms[u].astype(jnp.float32)
            for u in range(group):
                w = g * group + u
                new_walkers[q * width + w] = sums[u].astype(jnp.bfloat16)
                place = pl.ds(pl.multiple_of(w * electrons, electrons), electrons)
                for h in range(halves):
                    totals[h, place, :] = sums[u][:, h * 128 : (h + 1) * 128]

        def turn(d, carry):
            for e in range(elec):
                for h in range(halves):
                    low = e * orbitals + h * 128
                    nw_send[q, d, :, low : low + 128] = totals[
                        h, pl.ds(d * elec + e, width, stride=electrons), :
                    ].astype(jnp.bfloat16)
            return carry

        lax.fori_loop(0, blocks, turn, 0)
        exchange(me, blocks, nw_send, nw_recv, q, send_sems.at[2], recv_sems.at[2], land=place)

    def partial(q, half, target):
        left = nw_recv[q, pl.ds(half * pairs, pairs)].reshape(pairs * width, elec * orbitals)
        step = min(256, nchol)

        @pl.loop(0, nchol // step)
        def _(n):
            at = pl.ds(pl.multiple_of(n * step, step), step)
            target[:, at] = lax.dot_general(
                left, rotated[at, :], (((1,), (1,)), ((), ())), preferred_element_type=jnp.float32
            )

    def bias(q):
        partial(q, 1 - core, pair_send.at[q])
        across = pltpu.make_async_remote_copy(
            src_ref=pair_send.at[q],
            dst_ref=pair_recv.at[q],
            send_sem=send_sems.at[4, q],
            recv_sem=recv_sems.at[4, q],
            device_id={"chol": pair * 2 + 1 - core},
            device_id_type=MESH,
        )
        across.start()
        partial(q, core, pair_own)
        across.wait_recv()
        both = (pair_own[...] + pair_recv[q]).astype(jnp.bfloat16)
        fb_send[q] = both.reshape(pairs, width, nchol)

        def step(k, carry):
            peer = lax.rem(pair + k, pairs)
            pltpu.make_async_remote_copy(
                src_ref=fb_send.at[q, peer],
                dst_ref=fb_recv.at[q, pair],
                send_sem=send_sems.at[3, q],
                recv_sem=recv_sems.at[3, q],
                device_id={"chol": peer * 2 + core},
                device_id_type=MESH,
            ).start()
            return carry

        lax.fori_loop(1, pairs, step, 0)
        fb_recv[q, pair] = fb_send[q, pair]

    def finish(q):
        force_bias[q * width : (q + 1) * width, :] = lax.fori_loop(
            1,
            pairs,
            lambda s, acc: acc + fb_recv[q, s].astype(jnp.float32),
            fb_recv[q, 0].astype(jnp.float32),
        )

    for q in range(min(2, chunks)):
        send_operators(q)
    unfold(rotated_raw, rotated_wide, rotated)
    arrived(blocks, br_recv, 0, recv_sems.at[0])
    for q in range(chunks + 2):
        if q < chunks:
            if q + 2 < chunks:
                send_operators(q + 2)
            taylor(q)
        if 1 <= q <= chunks:
            arrived(blocks, nw_recv, q - 1, recv_sems.at[2])
            bias(q - 1)
        if q >= 2:
            arrived(pairs, fb_recv, q - 2, recv_sems.at[3])
            finish(q - 2)
    arrived(blocks, br_send, 0, send_sems.at[0])
    across.wait_send()
    pltpu.make_async_copy(same_core, same_core, field_sems.at[0]).wait()
    for q in range(chunks):
        arrived(blocks, op_send, q, send_sems.at[1])
        arrived(blocks, nw_send, q, send_sems.at[2])
        arrived(pairs, fb_send, q, send_sems.at[3])
        pltpu.make_async_copy(pair_send.at[q], pair_send.at[q], send_sems.at[4, q]).wait()


def shards(blocks, walkers, fields, chol_vectors, rotated, send_walker, slot_row):
    slots, electrons, orbitals = walkers.shape
    nchol, rows, _ = chol_vectors.shape
    elec = rotated.shape[1]
    cap = send_walker.shape[-1]
    width = min(chunk_slots, slots)
    chunks = slots // width
    dims = (blocks, chunks, width, cap, rows, elec)
    bf16, f32 = jnp.bfloat16, jnp.float32
    vmem, smem = (pl.BlockSpec(memory_space=m) for m in (pltpu.VMEM, pltpu.SMEM))
    return pl.pallas_call(
        functools.partial(kernel, dims),
        out_shape=(
            jax.ShapeDtypeStruct(walkers.shape, bf16),
            jax.ShapeDtypeStruct((slots, nchol), f32),
        ),
        in_specs=[smem, smem, vmem, vmem, pl.BlockSpec(memory_space=pl.ANY), vmem],
        out_specs=(vmem, vmem),
        scratch_shapes=[
            pltpu.VMEM(chol_vectors.shape, bf16),
            pltpu.VMEM((orbitals // 128, rows * unfold_depth, 128), f32),
            pltpu.VMEM((nchol, rows * orbitals), bf16),
            pltpu.VMEM((orbitals // 128, elec * unfold_depth, 128), f32),
            pltpu.VMEM((nchol, elec * orbitals), bf16),
            pltpu.VMEM((2, blocks // 2, slots, nchol), bf16),
            pltpu.VMEM((1, blocks, cap, electrons, orbitals), bf16),
            pltpu.VMEM((1, blocks, cap, electrons, orbitals), bf16),
            pltpu.VMEM((chunks, blocks, width, rows * orbitals), bf16),
            pltpu.VMEM((chunks, blocks, width, rows * orbitals), bf16),
            pltpu.VMEM((orbitals // 128, width * orbitals, 128), f32),
            pltpu.VMEM((orbitals // 128, width * electrons, 128), f32),
            pltpu.VMEM((chunks, blocks, width, elec * orbitals), bf16),
            pltpu.VMEM((chunks, blocks, width, elec * orbitals), bf16),
            pltpu.VMEM((chunks, blocks // 2 * width, nchol), f32),
            pltpu.VMEM((chunks, blocks // 2 * width, nchol), f32),
            pltpu.VMEM((blocks // 2 * width, nchol), f32),
            pltpu.VMEM((chunks, blocks // 2, width, nchol), bf16),
            pltpu.VMEM((chunks, blocks // 2, width, nchol), bf16),
            pltpu.SemaphoreType.DMA((5, chunks)),
            pltpu.SemaphoreType.DMA((5, chunks)),
            pltpu.SemaphoreType.DMA((4,)),
            pltpu.SemaphoreType.DMA,
            pltpu.SemaphoreType.DMA((chunks, math.gcd(4, blocks))),
        ],
        compiler_params=pltpu.CompilerParams(
            collective_id=0, has_side_effects=True, vmem_limit_bytes=60 * 1024 * 1024
        ),
    )(
        send_walker.reshape(-1),
        slot_row,
        walkers,
        fields,
        chol_vectors,
        rotated,
    )


def solution(mesh):
    in_specs = (
        P(("grp", "chol"), None, None),
        P(("grp", "chol"), None),
        P(None, "chol", None),
        P(None, "chol", None),
        P(("grp", "chol"), None, None),
        P(("grp", "chol")),
    )
    out_specs = (P(("grp", "chol"), None, None), P(("grp", "chol"), None))
    return jax.shard_map(
        functools.partial(shards, mesh.shape["chol"]),
        mesh=mesh,
        in_specs=in_specs,
        out_specs=out_specs,
        check_vma=False,
    )
```
